32 devices in a mesh: dp: 16 (over z, y, x), fsdp: 2 (over core).
Axes of the slice: x: 2, y: 2, z: 4, core: 2. Of those that a mesh axis runs over, the one named last changes fastest.
Arguments:
- enc_tokens: int32 [2, 32, 256], P(None, ('dp', 'fsdp')), may hold values from 0 to 4095
- dec_tokens: int32 [2, 32, 256], P(None, ('dp', 'fsdp')), may hold values from 0 to 4095
- targets: int32 [2, 32, 256], P(None, ('dp', 'fsdp')), may hold values from 0 to 4095
- segments: int32 [2, 32, 256], P(None, ('dp', 'fsdp')), may hold values from 0 to 3, never falling along the last dimension, each value on 1 to 200 neighbouring positions
- buckets: int32 [2, 256, 256], replicated, may hold values from 0 to 31
- step_count: int32 [1], replicated, may hold values from 1 to 20
- embedding: float32 [4096, 768], P('dp', 'fsdp'), may hold values from -6 to 6
- in_proj: float32 [3, 768, 2304], P(None, 'dp', 'fsdp'), may hold values from -0.21875 to 0.21875
- out_proj: float32 [3, 768, 768], P(None, 'dp', 'fsdp'), may hold values from -0.875 to 0.875
- ff_in: float32 [2, 768, 3072], P(None, 'dp', 'fsdp'), may hold values from -0.21875 to 0.21875
- ff_out: float32 [2, 3072, 768], P(None, 'dp', 'fsdp'), may hold values from -0.109375 to 0.109375
- small_params: float32 [768, 8], P('dp', 'fsdp'), may hold values from -1.5 to 1.5, as said below
- moment_embedding: float32 [4096, 768], P('dp', 'fsdp'), may hold values from -1.5258789e-05 to 1.5258789e-05
- moment_in_proj: float32 [3, 768, 2304], P(None, 'dp', 'fsdp'), may hold values from -1.5258789e-05 to 1.5258789e-05
- moment_out_proj: float32 [3, 768, 768], P(None, 'dp', 'fsdp'), may hold values from -1.5258789e-05 to 1.5258789e-05
- moment_ff_in: float32 [2, 768, 3072], P(None, 'dp', 'fsdp'), may hold values from -1.5258789e-05 to 1.5258789e-05
- moment_ff_out: float32 [2, 3072, 768], P(None, 'dp', 'fsdp'), may hold values from -1.5258789e-05 to 1.5258789e-05
- moment_small: float32 [768, 8], P('dp', 'fsdp'), may hold values from -1.5258789e-05 to 1.5258789e-05
- square_embedding: float32 [4096, 768], P('dp', 'fsdp'), may hold values from 1.5517194e-13 to 1.5517194e-12
- square_in_proj: float32 [3, 768, 2304], P(None, 'dp', 'fsdp'), may hold values from 1.5517194e-13 to 1.5517194e-12
- square_out_proj: float32 [3, 768, 768], P(None, 'dp', 'fsdp'), may hold values from 1.5517194e-13 to 1.5517194e-12
- square_ff_in: float32 [2, 768, 3072], P(None, 'dp', 'fsdp'), may hold values from 1.5517194e-13 to 1.5517194e-12
- square_ff_out: float32 [2, 3072, 768], P(None, 'dp', 'fsdp'), may hold values from 1.5517194e-13 to 1.5517194e-12
- square_small: float32 [768, 8], P('dp', 'fsdp'), may hold values from 1.5517194e-13 to 1.5517194e-12
Outputs:
- loss: float32 [], replicated
- grad_norm: float32 [], replicated
- new_moment_embedding: float32 [4096, 768], P('dp', 'fsdp')
- new_moment_in_proj: float32 [3, 768, 2304], P(None, 'dp', 'fsdp')
- new_moment_out_proj: float32 [3, 768, 768], P(None, 'dp', 'fsdp')
- new_moment_ff_in: float32 [2, 768, 3072], P(None, 'dp', 'fsdp')
- new_moment_ff_out: float32 [2, 3072, 768], P(None, 'dp', 'fsdp')
- new_moment_small: float32 [768, 8], P('dp', 'fsdp')
- new_square_embedding: float32 [4096, 768], P('dp', 'fsdp')
- new_square_in_proj: float32 [3, 768, 2304], P(None, 'dp', 'fsdp')
- new_square_out_proj: float32 [3, 768, 768], P(None, 'dp', 'fsdp')
- new_square_ff_in: float32 [2, 768, 3072], P(None, 'dp', 'fsdp')
- new_square_ff_out: float32 [2, 3072, 768], P(None, 'dp', 'fsdp')
- new_square_small: float32 [768, 8], P('dp', 'fsdp')
- change_embedding: float32 [4096, 768], P('dp', 'fsdp')
- change_in_proj: float32 [3, 768, 2304], P(None, 'dp', 'fsdp')
- change_out_proj: float32 [3, 768, 768], P(None, 'dp', 'fsdp')
- change_ff_in: float32 [2, 768, 3072], P(None, 'dp', 'fsdp')
- change_ff_out: float32 [2, 3072, 768], P(None, 'dp', 'fsdp')
- change_small: float32 [768, 8], P('dp', 'fsdp')
The draws below stay inside these ranges and needn't reach their ends.
Inputs may be any that keep to these rules, and one draw needn't show every extreme that they name: `segments`: along each sequence the ids never fall; a document holds 1 to 200 positions. `small_params`: columns 0 to 6 lie within 0.5 to 1.5.
All inputs are finite; a program needn't handle non-finite values.
Results may differ from the reference program's by a relative error of at most 0.011.
The reference program's roundings to bfloat16 on the way count: a program that leaves them out, or rounds other values in their place, can miss the bound.
Values may be sent and summed in bfloat16 or wider, within the bound.
No kernel may reach another device: no remote copies, remote signals or barrier semaphores. Data moves between devices by JAX's collectives and lax.ppermute only.
A program may use at most 384 MiB of HBM per device.

```python
import math
from functools import reduce
import jax
import jax.numpy as jnp
import numpy as np
from jax import lax

D = 768
H = 12
DH = 64
FF = 3072
V = 4096
NB = 32
L = 256
DOC_MAX = 200
SEGS = 4
MB = 2
SEQS_MB = 32
TOKENS = 16384
PARAMS = 19666944


def draw_small_params(key, part):
    first, second = jax.random.split(jax.random.fold_in(key, 11))
    gains = jax.random.uniform(first, (D, 7), jnp.float32, 0.6, 1.4)
    tables = jax.random.uniform(second, (D, 1), jnp.float32, -1.2, 1.2)
    return jnp.concatenate([gains, tables], axis=1)


def with_ends(result, own_key, least, largest):
    extent = result.shape
    index_at = [jax.random.randint(jax.random.fold_in(own_key, axis), (), 0, extent[axis]) for axis in range(len(extent))]
    result = result.at[tuple(index_at)].set(least)
    longest = extent.index(max(extent))
    index_at[longest] = (index_at[longest] + 1) % extent[longest]
    return result.at[tuple(index_at)].set(largest)


def block_levels(stream_key, dims, cuts, smallest, high):
    level = 1.0
    for axis_at, blocks in cuts:
        draws = jax.random.uniform(jax.random.fold_in(jax.random.fold_in(stream_key, 6), axis_at), (blocks,), jnp.float32, smallest / len(cuts), high / len(cuts))
        level = level * jnp.repeat(jnp.exp(draws), dims[axis_at] // blocks).reshape((-1,) + (1,) * (len(dims) - 1 - axis_at))
    return level


def cumulative_ranks(number_of, slope):
    loads = [(1 << 20) // math.isqrt(standing ** slope) + 1 for standing in range(1, number_of + 1)]
    deviation = 1 + sum(loads) // (1 << 30)
    return np.cumsum(np.array([max(1, weight // deviation) for weight in loads]))


def ranked_ids(stream_key, shape, amount, lean):
    listing = cumulative_ranks(amount, lean)
    lot = jax.random.randint(jax.random.fold_in(stream_key, 1), shape, 0, int(listing[amount - 1]))
    grade = jnp.searchsorted(jnp.asarray(listing, jnp.int32), lot, side="right")
    return jax.random.permutation(jax.random.fold_in(stream_key, 2), amount)[grade].astype(jnp.int32)


def length_profile(amount, total, reach, lean):
    portions = [(1 << 20) // math.isqrt(rank ** lean) + 1 for rank in range(2, amount + 1)]
    surplus, holding = total - reach - (amount - 1), [1] * (amount - 1)
    while surplus > 0:
        free = [i for i in range(amount - 1) if holding[i] < reach]
        whole, remaining = sum([portions[i] for i in free]), surplus
        for i in free:
            addition = min(reach - holding[i], max(1, remaining * portions[i] // whole), surplus)
            holding[i] = holding[i] + addition
            surplus = surplus - addition
    return np.array([reach] + holding)


def uneven(key, amount, total, bound, lean):
    if amount == 2:
        one = jax.random.randint(key, (), max(1, total - bound), min(bound, total - 1) + 1)
        return jnp.stack([one, total - one])
    sizes = jnp.asarray(length_profile(amount, total, bound, lean), jnp.int32)
    twos = (amount - 1) // 2
    donor, sink = sizes[1:1 + 2 * twos:2], sizes[2:2 + 2 * twos:2]
    room = jnp.minimum(donor - 1, bound - sink)
    shifted = jax.random.randint(jax.random.fold_in(key, 1), (twos,), 0, 1 << 20) % (room + 1)
    sizes = sizes.at[1:1 + 2 * twos:2].set(donor - shifted).at[2:2 + 2 * twos:2].set(sink + shifted)
    return sizes[jax.random.permutation(jax.random.fold_in(key, 2), amount)]


def scatter_about(key, dims, spread, limit, cuts=(), held_as=jnp.bfloat16):
    result = spread * jax.random.normal(key, dims, jnp.float32)
    if cuts:
        result = result * block_levels(key, dims, cuts, -0.22, 0.18)
    return jnp.clip(result, -limit, limit).astype(held_as)


def setup_inputs(seed: int = 0) -> dict:
    key_list = jax.random.split(jax.random.key(seed), 25)
    return {
        "enc_tokens": with_ends(ranked_ids(key_list[0], (MB, SEQS_MB, L), V, 2), jax.random.fold_in(key_list[0], 3), 0, V - 1).astype(jnp.int32),
        "dec_tokens": with_ends(ranked_ids(key_list[1], (MB, SEQS_MB, L), V, 2), jax.random.fold_in(key_list[1], 3), 0, V - 1).astype(jnp.int32),
        "targets": with_ends(jax.random.randint(key_list[2], (MB, SEQS_MB, L), 0, V), jax.random.fold_in(key_list[2], 1), 0, V - 1).astype(jnp.int32),
        "segments": jax.vmap(lambda own: jnp.searchsorted(jnp.cumsum(uneven(own, SEGS, L, DOC_MAX, 1)), jnp.arange(L), side="right"))(jax.random.split(key_list[3], MB * SEQS_MB)).reshape((MB, SEQS_MB, L)).astype(jnp.int32),
        "buckets": with_ends(jax.random.randint(key_list[4], (2, L, L), 0, NB), jax.random.fold_in(key_list[4], 1), 0, NB - 1).astype(jnp.int32),
        "step_count": jax.random.randint(key_list[5], (1,), 1, 21).astype(jnp.int32),
        "embedding": scatter_about(key_list[6], (V, D), 1.0, 6.0, ((0, 16), (1, 2)), jnp.float32),
        "in_proj": scatter_about(key_list[7], (3, D, 3 * D), D ** -0.5, 0.21875, ((1, 16), (2, 2)), jnp.float32),
        "out_proj": scatter_about(key_list[8], (3, D, D), (D // 16) ** -0.5, 0.875, ((1, 16), (2, 2)), jnp.float32),
        "ff_in": scatter_about(key_list[9], (2, D, FF), D ** -0.5, 0.21875, ((1, 16), (2, 2)), jnp.float32),
        "ff_out": scatter_about(key_list[10], (2, FF, D), FF ** -0.5, 0.109375, ((1, 16), (2, 2)), jnp.float32),
        "small_params": draw_small_params(jax.random.fold_in(key_list[24], 71), 0),
        "moment_embedding": scatter_about(key_list[12], (V, D), (TOKENS * PARAMS // 2) ** -0.5, 1.52587890625e-05, ((0, 16), (1, 2)), jnp.float32),
        "moment_in_proj": scatter_about(key_list[13], (3, D, 3 * D), (TOKENS * PARAMS // 2) ** -0.5, 1.52587890625e-05, ((1, 16), (2, 2)), jnp.float32),
        "moment_out_proj": scatter_about(key_list[14], (3, D, D), (TOKENS * PARAMS // 2) ** -0.5, 1.52587890625e-05, ((1, 16), (2, 2)), jnp.float32),
        "moment_ff_in": scatter_about(key_list[15], (2, D, FF), (TOKENS * PARAMS // 2) ** -0.5, 1.52587890625e-05, ((1, 16), (2, 2)), jnp.float32),
        "moment_ff_out": scatter_about(key_list[16], (2, FF, D), (TOKENS * PARAMS // 2) ** -0.5, 1.52587890625e-05, ((1, 16), (2, 2)), jnp.float32),
        "moment_small": scatter_about(key_list[17], (D, 8), (TOKENS * PARAMS // 2) ** -0.5, 1.52587890625e-05, ((0, 16), (1, 2)), jnp.float32),
        "square_embedding": jnp.clip(jnp.exp(math.log(1.55171936497972e-12) - 2.3025851 * jax.random.uniform(key_list[18], (V, D), jnp.float32) ** block_levels(key_list[18], (V, D), ((0, 16), (1, 2)), -0.2, 0.2)), 1.55171936497972e-13, 1.55171936497972e-12),
        "square_in_proj": jnp.clip(jnp.exp(math.log(1.55171936497972e-12) - 2.3025851 * jax.random.uniform(key_list[19], (3, D, 3 * D), jnp.float32) ** block_levels(key_list[19], (3, D, 3 * D), ((1, 16), (2, 2)), -0.2, 0.2)), 1.55171936497972e-13, 1.55171936497972e-12),
        "square_out_proj": jnp.clip(jnp.exp(math.log(1.55171936497972e-12) - 2.3025851 * jax.random.uniform(key_list[20], (3, D, D), jnp.float32) ** block_levels(key_list[20], (3, D, D), ((1, 16), (2, 2)), -0.2, 0.2)), 1.55171936497972e-13, 1.55171936497972e-12),
        "square_ff_in": jnp.clip(jnp.exp(math.log(1.55171936497972e-12) - 2.3025851 * jax.random.uniform(key_list[21], (2, D, FF), jnp.float32) ** block_levels(key_list[21], (2, D, FF), ((1, 16), (2, 2)), -0.2, 0.2)), 1.55171936497972e-13, 1.55171936497972e-12),
        "square_ff_out": jnp.clip(jnp.exp(math.log(1.55171936497972e-12) - 2.3025851 * jax.random.uniform(key_list[22], (2, FF, D), jnp.float32) ** block_levels(key_list[22], (2, FF, D), ((1, 16), (2, 2)), -0.2, 0.2)), 1.55171936497972e-13, 1.55171936497972e-12),
        "square_small": jnp.clip(jnp.exp(math.log(1.55171936497972e-12) - 2.3025851 * jax.random.uniform(key_list[23], (D, 8), jnp.float32) ** block_levels(key_list[23], (D, 8), ((0, 16), (1, 2)), -0.2, 0.2)), 1.55171936497972e-13, 1.55171936497972e-12),
    }


@jax.custom_vjp
def low(v):
    return lax.optimization_barrier(v.astype(jnp.bfloat16)).astype(jnp.float32)

@jax.custom_vjp
def low_back(v):
    return v

def low_keep(v):
    return (low(v), None)

def low_pass(kept, grad):
    return (grad,)

def back_keep(v):
    return (v, None)

def back_low(kept, grad):
    return (low(grad),)
low.defvjp(low_keep, low_pass)
low_back.defvjp(back_keep, back_low)
highest = lax.Precision.HIGHEST
norm_eps = 1e-06
smooth = 0.1
zcoef = 0.01
clip_scale = 14.0
beta_one = 0.9
beta_two = 0.999
adam_eps = 1e-08

def matmul(left, right):
    return jnp.dot(left, right, precision=highest)

def rms_norm(hidden, gain):
    return hidden * lax.rsqrt(lax.optimization_barrier(jnp.mean(hidden * hidden, axis=-1, keepdims=True)) + norm_eps) * gain

def attend(queries, key_rows, values, bias, mask):
    raw = low_back(jnp.einsum('sqhd,skhd->shqk', queries, key_rows, precision=highest))
    scores = jnp.where(mask[:, None], raw * DH ** (-0.5) + bias, -1e+30)
    top = lax.optimization_barrier(jnp.max(scores, axis=-1, keepdims=True))
    logsum = top + jnp.log(lax.optimization_barrier(jnp.sum(jnp.exp(scores - top), axis=-1, keepdims=True)))
    probs = low(jnp.exp(scores - logsum))
    return low(low_back(jnp.einsum('shqk,skhd->sqhd', probs, values, precision=highest)))

def heads(packed, index):
    return packed[..., index * D:(index + 1) * D].reshape(packed.shape[0], packed.shape[1], H, DH)

def self_layer(hidden, weights, gain, bias, mask):
    normed = low(rms_norm(hidden, gain))
    packed = low(low_back(matmul(normed, weights[0])))
    mixed = attend(heads(packed, 0), heads(packed, 1), heads(packed, 2), bias, mask)
    return hidden + low_back(matmul(mixed.reshape(hidden.shape), weights[1]))

def feed_layer(hidden, weights, gain):
    normed = low(rms_norm(hidden, gain))
    inner = low_back(matmul(normed, weights[0]))
    active = low(jnp.maximum(inner, 0.0))
    return hidden + low_back(matmul(active, weights[1]))

def block_loss(params, enc_ids, dec_ids, target_ids, segment_ids, buckets):
    embed, in_side, out_side, up_side, down_side, small = [low(weight) for weight in params]
    gains = small[:, :7]
    tables = small[:, 7].reshape(2, NB, H)
    bias_enc = jnp.transpose(tables[0][buckets[0]], (2, 0, 1))
    bias_dec = jnp.transpose(tables[1][buckets[1]], (2, 0, 1))
    same = segment_ids[:, :, None] == segment_ids[:, None, :]
    lower = jnp.arange(L)[:, None] >= jnp.arange(L)[None, :]
    causal = jnp.logical_and(same, lower[None])
    encoder = jnp.take(embed, enc_ids, axis=0)
    encoder = self_layer(encoder, (in_side[0], out_side[0]), gains[:, 0], bias_enc, same)
    encoder = feed_layer(encoder, (up_side[0], down_side[0]), gains[:, 1])
    encoded = low(rms_norm(encoder, gains[:, 2]))
    decoder = jnp.take(embed, dec_ids, axis=0)
    decoder = self_layer(decoder, (in_side[1], out_side[1]), gains[:, 3], bias_dec, causal)
    normed = low(rms_norm(decoder, gains[:, 4]))
    queries = low(low_back(matmul(normed, in_side[2][:, :D])))
    pairs = low(low_back(matmul(encoded, in_side[2][:, D:])))
    mixed = attend(queries.reshape(queries.shape[0], L, H, DH), heads(pairs, 0), heads(pairs, 1), 0.0, same)
    decoder = decoder + low_back(matmul(mixed.reshape(decoder.shape), out_side[2]))
    decoder = feed_layer(decoder, (up_side[1], down_side[1]), gains[:, 5])
    final = low(rms_norm(decoder, gains[:, 6]))
    logits = low_back(matmul(final, embed.T)) * D ** (-0.5)
    top = lax.optimization_barrier(jnp.max(logits, axis=-1, keepdims=True))
    logsum = (top + jnp.log(lax.optimization_barrier(jnp.sum(jnp.exp(logits - top), axis=-1, keepdims=True))))[..., 0]
    picked = lax.optimization_barrier(jnp.sum(jnp.where(jnp.arange(V) == target_ids[..., None], logits, 0.0), axis=-1))
    per_token = logsum - (1.0 - smooth) * picked - smooth * lax.optimization_barrier(jnp.mean(logits, axis=-1)) + zcoef * logsum * logsum
    return jnp.sum(per_token)

def adam_step(weight, moment, square, gradient, factor, rate, decay, first_fix, second_fix):
    clipped = gradient * factor
    new_moment = beta_one * moment + (1.0 - beta_one) * clipped
    new_square = beta_two * square + (1.0 - beta_two) * clipped * clipped
    change = -rate * (new_moment / first_fix / (jnp.sqrt(new_square / second_fix) + adam_eps) + decay * weight)
    return (new_moment, new_square, change)

def reference(enc_tokens, dec_tokens, targets, segments, buckets, step_count, embedding, in_proj, out_proj, ff_in, ff_out, small_params, moment_embedding, moment_in_proj, moment_out_proj, moment_ff_in, moment_ff_out, moment_small, square_embedding, square_in_proj, square_out_proj, square_ff_in, square_ff_out, square_small):
    params = (embedding, in_proj, out_proj, ff_in, ff_out, small_params)
    count = MB * SEQS_MB
    total = count * L
    block = math.gcd(16, count)

    def fold(ids):
        return ids.reshape(count // block, block, L)
    batches = (fold(enc_tokens), fold(dec_tokens), fold(targets), fold(segments))

    def one_block(carry, batch):
        loss_sum, grads = carry
        value, pull = jax.vjp(lambda weights: block_loss(weights, batch[0], batch[1], batch[2], batch[3], buckets), params)
        parts, = pull(jnp.float32(1.0 / total))
        return ((loss_sum + value, jax.tree.map(jnp.add, grads, parts)), None)
    start = (jnp.float32(0.0), jax.tree.map(jnp.zeros_like, params))
    (loss_sum, grads), unused = lax.scan(one_block, start, batches)
    loss = loss_sum / total
    norm = jnp.sqrt(reduce(jnp.add, [jnp.sum(gradient * gradient) for gradient in grads]))
    factor = jnp.minimum(1.0, clip_scale / math.sqrt(total) / (norm + 1e-06))
    rates = (0.5, 0.5 / math.sqrt(D), 2.0 / math.sqrt(D), 0.5 / math.sqrt(D), 0.5 / math.sqrt(FF), 0.05)
    decays = (0.1, 0.1, 0.1, 0.1, 0.1, 0.0)
    moments = (moment_embedding, moment_in_proj, moment_out_proj, moment_ff_in, moment_ff_out, moment_small)
    squares = (square_embedding, square_in_proj, square_out_proj, square_ff_in, square_ff_out, square_small)
    steps_done = step_count[0].astype(jnp.float32)
    first_fix = 1.0 - jnp.power(jnp.float32(beta_one), steps_done)
    second_fix = 1.0 - jnp.power(jnp.float32(beta_two), steps_done)
    results = [adam_step(params[index], moments[index], squares[index], grads[index], factor, rates[index], decays[index], first_fix, second_fix) for index in range(6)]
    return (loss, norm, results[0][0], results[1][0], results[2][0], results[3][0], results[4][0], results[5][0], results[0][1], results[1][1], results[2][1], results[3][1], results[4][1], results[5][1], results[0][2], results[1][2], results[2][2], results[3][2], results[4][2], results[5][2])
```

```python
from functools import partial
from functools import reduce
import math

import jax
import jax.numpy as jnp
from jax import lax
from jax.sharding import PartitionSpec as P

D = 768
H = 12
DH = 64
FF = 3072
NB = 32


norm_eps = 1e-06
smooth = 0.1
zcoef = 0.01
clip_scale = 14.0
beta_one = 0.9
beta_two = 0.999
adam_eps = 1e-08


def rms_norm(hidden, gain):
    return hidden * lax.rsqrt(jnp.mean(hidden * hidden, axis=-1, keepdims=True) + norm_eps) * gain


def norm_back(hidden, gain, upstream):
    unused, pull = jax.vjp(rms_norm, hidden, gain)
    return pull(upstream)


def matmul(left, right):
    return jnp.dot(left, right, preferred_element_type=jnp.float32)


def weight_grad(left, upstream):
    return lax.dot_general(
        left, upstream, (((0,), (0,)), ((), ())), preferred_element_type=jnp.float32
    )


def input_grad(upstream, weight):
    return lax.dot_general(
        upstream, weight, (((1,), (1,)), ((), ())), preferred_element_type=jnp.float32
    )


def split_heads(packed, index, shape):
    width = shape[2] * shape[3]
    return packed[:, index * width : (index + 1) * width].reshape(shape)


def score_block(queries, key_rows, bias, mask):
    raw = jnp.einsum("sqhd,skhd->shqk", queries, key_rows, preferred_element_type=jnp.float32)
    return jnp.where(mask[:, None], raw * queries.shape[-1] ** (-0.5) + bias, -1e30)


def attend_forward(queries, key_rows, values, bias, mask):
    scores = score_block(queries, key_rows, bias, mask)
    top = jnp.max(scores, axis=-1, keepdims=True)
    logsum = top + jnp.log(jnp.sum(jnp.exp(scores - top), axis=-1, keepdims=True))
    probs = jnp.exp(scores - logsum).astype(jnp.bfloat16)
    mixed = jnp.einsum("shqk,skhd->sqhd", probs, values, preferred_element_type=jnp.float32)
    return (mixed.astype(jnp.bfloat16), logsum)


def attend_backward(queries, key_rows, values, bias, mask, logsum, d_mixed):
    scores = score_block(queries, key_rows, bias, mask)
    probs = jnp.exp(scores - logsum)
    d_probs = jnp.einsum("sqhd,skhd->shqk", d_mixed, values, preferred_element_type=jnp.float32)
    d_scores = probs * (d_probs - jnp.sum(probs * d_probs, axis=-1, keepdims=True))
    d_raw = (d_scores * queries.shape[-1] ** (-0.5)).astype(jnp.bfloat16)
    d_queries = jnp.einsum("shqk,skhd->sqhd", d_raw, key_rows, preferred_element_type=jnp.float32)
    d_keys = jnp.einsum("shqk,sqhd->skhd", d_raw, queries, preferred_element_type=jnp.float32)
    d_values = jnp.einsum(
        "shqk,sqhd->skhd", probs.astype(jnp.bfloat16), d_mixed, preferred_element_type=jnp.float32
    )
    return (d_queries, d_keys, d_values, jnp.sum(d_scores, axis=0))


def self_forward(hidden, weights, gain, bias, mask, shape):
    normed = rms_norm(hidden, gain).astype(jnp.bfloat16)
    packed = matmul(normed, weights[0]).astype(jnp.bfloat16)
    mixed, logsum = attend_forward(
        split_heads(packed, 0, shape),
        split_heads(packed, 1, shape),
        split_heads(packed, 2, shape),
        bias,
        mask,
    )
    flat = mixed.reshape(hidden.shape)
    return (hidden + matmul(flat, weights[1]), (normed, packed, flat, logsum))


def self_backward(hidden, saved, weights, gain, bias, mask, shape, d_hidden):
    normed, packed, flat, logsum = saved
    d_out = d_hidden.astype(jnp.bfloat16)
    grad_out = weight_grad(flat, d_out)
    d_mixed = input_grad(d_out, weights[1]).astype(jnp.bfloat16).reshape(shape)
    d_queries, d_keys, d_values, d_bias = attend_backward(
        split_heads(packed, 0, shape),
        split_heads(packed, 1, shape),
        split_heads(packed, 2, shape),
        bias,
        mask,
        logsum,
        d_mixed,
    )
    d_packed = jnp.concatenate(
        [d_queries.reshape(flat.shape), d_keys.reshape(flat.shape), d_values.reshape(flat.shape)],
        axis=1,
    ).astype(jnp.bfloat16)
    grad_in = weight_grad(normed, d_packed)
    d_input, d_gain = norm_back(hidden, gain, input_grad(d_packed, weights[0]))
    return (d_hidden + d_input, grad_in, grad_out, d_gain, d_bias)


def cross_forward(hidden, encoded, weights, gain, mask, shape):
    width = hidden.shape[1]
    normed = rms_norm(hidden, gain).astype(jnp.bfloat16)
    queries = matmul(normed, weights[0][:, :width]).astype(jnp.bfloat16)
    pairs = matmul(encoded, weights[0][:, width:]).astype(jnp.bfloat16)
    mixed, logsum = attend_forward(
        queries.reshape(shape),
        split_heads(pairs, 0, shape),
        split_heads(pairs, 1, shape),
        0.0,
        mask,
    )
    flat = mixed.reshape(hidden.shape)
    return (hidden + matmul(flat, weights[1]), (normed, queries, pairs, flat, logsum))


def cross_backward(hidden, encoded, saved, weights, gain, mask, shape, d_hidden):
    normed, queries, pairs, flat, logsum = saved
    width = hidden.shape[1]
    d_out = d_hidden.astype(jnp.bfloat16)
    grad_out = weight_grad(flat, d_out)
    d_mixed = input_grad(d_out, weights[1]).astype(jnp.bfloat16).reshape(shape)
    d_queries, d_keys, d_values, unused = attend_backward(
        queries.reshape(shape),
        split_heads(pairs, 0, shape),
        split_heads(pairs, 1, shape),
        0.0,
        mask,
        logsum,
        d_mixed,
    )
    d_query_rows = d_queries.reshape(flat.shape).astype(jnp.bfloat16)
    d_pairs = jnp.concatenate(
        [d_keys.reshape(flat.shape), d_values.reshape(flat.shape)], axis=1
    ).astype(jnp.bfloat16)
    grad_in = jnp.concatenate(
        [weight_grad(normed, d_query_rows), weight_grad(encoded, d_pairs)], axis=1
    )
    d_encoded = input_grad(d_pairs, weights[0][:, width:])
    d_input, d_gain = norm_back(hidden, gain, input_grad(d_query_rows, weights[0][:, :width]))
    return (d_hidden + d_input, d_encoded, grad_in, grad_out, d_gain)


def feed_forward(hidden, weights, gain):
    normed = rms_norm(hidden, gain).astype(jnp.bfloat16)
    active = jnp.maximum(matmul(normed, weights[0]), 0.0).astype(jnp.bfloat16)
    return (hidden + matmul(active, weights[1]), (normed, active))


def feed_backward(hidden, saved, weights, gain, d_hidden):
    normed, active = saved
    d_out = d_hidden.astype(jnp.bfloat16)
    grad_down = weight_grad(active, d_out)
    d_inner = jnp.where(active > 0, input_grad(d_out, weights[1]), 0.0).astype(jnp.bfloat16)
    grad_up = weight_grad(normed, d_inner)
    d_input, d_gain = norm_back(hidden, gain, input_grad(d_inner, weights[0]))
    return (d_hidden + d_input, grad_up, grad_down, d_gain)


def token_losses(logits, target_ids):
    top = jnp.max(logits, axis=-1, keepdims=True)
    logsum = (top + jnp.log(jnp.sum(jnp.exp(logits - top), axis=-1, keepdims=True)))[:, 0]
    picked = jnp.sum(
        jnp.where(jnp.arange(logits.shape[1])[None, :] == target_ids[:, None], logits, 0.0), axis=-1
    )
    return jnp.sum(
        logsum
        - (1.0 - smooth) * picked
        - smooth * jnp.mean(logits, axis=-1)
        + zcoef * logsum * logsum
    )


def bucket_hot(bucket_ids, count):
    return (jnp.arange(count)[:, None] == bucket_ids.reshape(1, -1)).astype(jnp.bfloat16)


def position_bias(onehot, table, length):
    bias = lax.dot_general(
        table, onehot, (((0,), (0,)), ((), ())), preferred_element_type=jnp.float32
    )
    return bias.reshape(table.shape[1], length, length)


def high_low(values):
    high = values.astype(jnp.bfloat16)
    low = (values - high.astype(jnp.float32)).astype(jnp.bfloat16)
    return (high, low)


def table_grad(onehot, d_bias):
    flat = d_bias.reshape(d_bias.shape[0], -1)
    high, low = high_low(flat)
    both = jnp.concatenate([high, low], axis=0)
    sums = lax.dot_general(
        onehot, both, (((1,), (1,)), ((), ())), preferred_element_type=jnp.float32
    )
    return sums[:, : flat.shape[0]] + sums[:, flat.shape[0] :]


def pack_columns(shard, width):
    rows, columns = shard.shape
    if columns == width:
        return [shard]
    return [shard[:, at : at + width] for at in range(0, columns, width)]


def gather_weights(shards, small):
    width = shards[0].shape[1]
    pieces = []
    for shard in shards:
        pieces.extend(pack_columns(shard.astype(jnp.bfloat16), width))
    tail = small.astype(jnp.bfloat16).reshape(1, -1)
    tail = jnp.pad(tail, ((0, 15), (0, width - tail.shape[1])))
    packed = jnp.concatenate(pieces + [tail], axis=0)
    ways = (lax.axis_size("dp"), lax.axis_size("fsdp"))
    full = lax.all_gather(packed, ("dp", "fsdp"), axis=0, tiled=False)
    full = full.reshape(ways + packed.shape)
    weights = []
    start = 0
    for shard in shards:
        rows, columns = shard.shape
        count = columns // width
        part = full[:, :, start : start + rows * count]
        start += rows * count
        part = part.reshape(ways + (count, rows, width)).transpose(0, 3, 1, 2, 4)
        weights.append(part.reshape(ways[0] * rows, ways[1] * columns))
    last = full[:, :, start, : small.size].reshape(ways + small.shape)
    last = last.transpose(0, 2, 1, 3).reshape(ways[0] * small.shape[0], ways[1] * small.shape[1])
    return (weights, last)


def exchange(values, axis, bit):
    size = lax.axis_size(axis)
    return lax.ppermute(values, axis, [(at, at ^ (1 << bit)) for at in range(size)])


def scatter_sum(gradient, order_of, link=jnp.bfloat16):
    rows, columns = gradient.shape
    half = columns // 2
    core = lax.axis_index("fsdp")
    place = lax.axis_index("dp")
    bits = lax.axis_size("dp").bit_length() - 1
    sent = lax.dynamic_slice(gradient, (0, (1 - core) * half), (rows, half)).astype(link)
    kept = lax.dynamic_slice(gradient, (0, core * half), (rows, half)).astype(jnp.float32)
    total = kept + exchange(sent, "fsdp", 0).astype(jnp.float32)
    total = total.reshape((2,) * bits + (rows >> bits, half))
    left = list(range(bits - 1, -1, -1))
    for bit in order_of(bits):
        axis = left.index(bit)
        mine = (place >> bit) & 1
        sent = lax.dynamic_index_in_dim(total, 1 - mine, axis, keepdims=False).astype(link)
        kept = lax.dynamic_index_in_dim(total, mine, axis, keepdims=False)
        total = kept + exchange(sent, "dp", bit).astype(jnp.float32)
        left.pop(axis)
    return total


def order_even(bits):
    return list(range(bits))


def order_odd(bits):
    return [1, 0] + list(range(2, bits))


def adam_step(weight, moment, square, gradient, factor, rate, decay, first_fix, second_fix):
    clipped = gradient * factor
    new_moment = beta_one * moment + (1.0 - beta_one) * clipped
    new_square = beta_two * square + (1.0 - beta_two) * clipped * clipped
    change = -rate * (
        new_moment / first_fix / (jnp.sqrt(new_square / second_fix) + adam_eps) + decay * weight
    )
    return (new_moment, new_square, change)


def per_device(
    enc_tokens,
    dec_tokens,
    targets,
    segments,
    buckets,
    step_count,
    embedding,
    in_proj,
    out_proj,
    ff_in,
    ff_out,
    small_params,
    moment_embedding,
    moment_in_proj,
    moment_out_proj,
    moment_ff_in,
    moment_ff_out,
    moment_small,
    square_embedding,
    square_in_proj,
    square_out_proj,
    square_ff_in,
    square_ff_out,
    square_small,
):
    micro_count, seq_count, length = enc_tokens.shape
    total = micro_count * seq_count * length * lax.axis_size("dp") * lax.axis_size("fsdp")
    sequences = micro_count * seq_count
    shape = (sequences, length, H, DH)
    shards = [
        embedding,
        in_proj[0],
        out_proj[0],
        ff_in[0],
        ff_out[0],
        in_proj[1],
        out_proj[1],
        in_proj[2],
        out_proj[2],
        ff_in[1],
        ff_out[1],
    ]
    weights, small_full = gather_weights(shards, small_params)
    embed_full = weights[0]
    self_enc = (weights[1], weights[2])
    feed_enc = (weights[3], weights[4])
    self_dec = (weights[5], weights[6])
    cross_dec = (weights[7], weights[8])
    feed_dec = (weights[9], weights[10])
    gains = small_full[:, :7].astype(jnp.float32)
    tables = small_full[:, 7].reshape(2, NB, H)
    hot_enc = bucket_hot(buckets[0], NB)
    hot_dec = bucket_hot(buckets[1], NB)
    lower = jnp.arange(length)[:, None] >= jnp.arange(length)[None, :]
    scale = D ** (-0.5)
    enc_ids = enc_tokens.reshape(-1)
    dec_ids = dec_tokens.reshape(-1)
    target_ids = targets.reshape(-1)
    seg_ids = segments.reshape(sequences, length)
    same = seg_ids[:, :, None] == seg_ids[:, None, :]
    causal = jnp.logical_and(same, lower[None])
    bias_enc = position_bias(hot_enc, tables[0], length)
    bias_dec = position_bias(hot_dec, tables[1], length)
    vocabulary = embed_full.shape[0]
    both_ids = jnp.concatenate([enc_ids, dec_ids])
    both_hot = (both_ids[:, None] == jnp.arange(vocabulary)[None, :]).astype(jnp.bfloat16)
    rows0 = matmul(both_hot, embed_full)
    encode0 = rows0[: enc_ids.shape[0]]
    decode0 = rows0[enc_ids.shape[0] :]
    encode1, saved1 = self_forward(encode0, self_enc, gains[:, 0], bias_enc, same, shape)
    encode2, saved2 = feed_forward(encode1, feed_enc, gains[:, 1])
    encoded = rms_norm(encode2, gains[:, 2]).astype(jnp.bfloat16)
    decode1, saved3 = self_forward(decode0, self_dec, gains[:, 3], bias_dec, causal, shape)
    decode2, saved4 = cross_forward(decode1, encoded, cross_dec, gains[:, 4], same, shape)
    decode3, saved5 = feed_forward(decode2, feed_dec, gains[:, 5])
    final = rms_norm(decode3, gains[:, 6]).astype(jnp.bfloat16)
    logits = input_grad(final, embed_full) * scale
    loss_part, pull = jax.vjp(partial(token_losses, target_ids=target_ids), logits)
    loss_local = loss_part / total
    d_raw = (pull(jnp.float32(1.0 / total))[0] * scale).astype(jnp.bfloat16)
    d_decode3, d_gain6 = norm_back(decode3, gains[:, 6], matmul(d_raw, embed_full))
    d_decode2, grad_up5, grad_down5, d_gain5 = feed_backward(
        decode2, saved5, feed_dec, gains[:, 5], d_decode3
    )
    done_up5 = scatter_sum(grad_up5, order_even)
    done_down5 = scatter_sum(grad_down5, order_odd)
    d_decode1, d_encoded, grad_in4, grad_out4, d_gain4 = cross_backward(
        decode1, encoded, saved4, cross_dec, gains[:, 4], same, shape, d_decode2
    )
    done_in4 = scatter_sum(grad_in4, order_even)
    done_out4 = scatter_sum(grad_out4, order_odd)
    d_decode0, grad_in3, grad_out3, d_gain3, d_bias_dec = self_backward(
        decode0, saved3, self_dec, gains[:, 3], bias_dec, causal, shape, d_decode1
    )
    done_in3 = scatter_sum(grad_in3, order_odd)
    done_out3 = scatter_sum(grad_out3, order_even)
    d_encode2, d_gain2 = norm_back(encode2, gains[:, 2], d_encoded)
    d_encode1, grad_up2, grad_down2, d_gain1 = feed_backward(
        encode1, saved2, feed_enc, gains[:, 1], d_encode2
    )
    done_up2 = scatter_sum(grad_up2, order_even)
    done_down2 = scatter_sum(grad_down2, order_odd)
    d_encode0, grad_in1, grad_out1, d_gain0, d_bias_enc = self_backward(
        encode0, saved1, self_enc, gains[:, 0], bias_enc, same, shape, d_encode1
    )
    done_in1 = scatter_sum(grad_in1, order_even)
    done_out1 = scatter_sum(grad_out1, order_odd)
    d_rows = jnp.concatenate([d_encode0, d_decode0], axis=0)
    d_high, d_low = high_low(d_rows)
    grad_embed = weight_grad(
        jnp.concatenate([d_raw, both_hot, both_hot], axis=0),
        jnp.concatenate([final, d_high, d_low], axis=0),
    )
    done_embed = scatter_sum(grad_embed, order_even)
    grad_tables = jnp.concatenate(
        [
            table_grad(hot_enc, d_bias_enc).reshape(-1),
            table_grad(hot_dec, d_bias_dec).reshape(-1),
        ]
    )
    grad_small = jnp.stack(
        [d_gain0, d_gain1, d_gain2, d_gain3, d_gain4, d_gain5, d_gain6, grad_tables], axis=0
    )
    small_sum, loss_total = lax.psum((grad_small, loss_local), ("dp", "fsdp"))
    small_rows, small_columns = small_params.shape
    done_small = lax.dynamic_slice(
        small_sum,
        (lax.axis_index("fsdp") * small_columns, lax.axis_index("dp") * small_rows),
        (small_columns, small_rows),
    ).T
    grads = (
        done_embed.reshape(embedding.shape),
        jnp.stack([done_in1, done_in3, done_in4]),
        jnp.stack([done_out1, done_out3, done_out4]),
        jnp.stack([done_up2, done_up5]),
        jnp.stack([done_down2, done_down5]),
        done_small,
    )
    squares_local = reduce(jnp.add, [jnp.sum(gradient * gradient) for gradient in grads])
    squares_total = lax.psum(squares_local, ("dp", "fsdp"))
    grad_norm = jnp.sqrt(squares_total)
    factor = jnp.minimum(1.0, clip_scale / math.sqrt(total) / (grad_norm + 1e-06))
    masters = (embedding, in_proj, out_proj, ff_in, ff_out, small_params)
    moments = (
        moment_embedding,
        moment_in_proj,
        moment_out_proj,
        moment_ff_in,
        moment_ff_out,
        moment_small,
    )
    squares = (
        square_embedding,
        square_in_proj,
        square_out_proj,
        square_ff_in,
        square_ff_out,
        square_small,
    )
    rates = (
        0.5,
        0.5 / math.sqrt(D),
        2.0 / math.sqrt(D),
        0.5 / math.sqrt(D),
        0.5 / math.sqrt(FF),
        0.05,
    )
    decays = (0.1, 0.1, 0.1, 0.1, 0.1, 0.0)
    steps_done = step_count[0].astype(jnp.float32)
    first_fix = 1.0 - jnp.power(jnp.float32(beta_one), steps_done)
    second_fix = 1.0 - jnp.power(jnp.float32(beta_two), steps_done)
    results = [
        adam_step(
            masters[index],
            moments[index],
            squares[index],
            grads[index],
            factor,
            rates[index],
            decays[index],
            first_fix,
            second_fix,
        )
        for index in range(6)
    ]
    return (
        loss_total,
        grad_norm,
        results[0][0],
        results[1][0],
        results[2][0],
        results[3][0],
        results[4][0],
        results[5][0],
        results[0][1],
        results[1][1],
        results[2][1],
        results[3][1],
        results[4][1],
        results[5][1],
        results[0][2],
        results[1][2],
        results[2][2],
        results[3][2],
        results[4][2],
        results[5][2],
    )


def solution(mesh):
    placed = (
        P(None, ("dp", "fsdp"), None),
        P(None, ("dp", "fsdp"), None),
        P(None, ("dp", "fsdp"), None),
        P(None, ("dp", "fsdp"), None),
        P(),
        P(),
        P("dp", "fsdp"),
        P(None, "dp", "fsdp"),
        P(None, "dp", "fsdp"),
        P(None, "dp", "fsdp"),
        P(None, "dp", "fsdp"),
        P("dp", "fsdp"),
        P("dp", "fsdp"),
        P(None, "dp", "fsdp"),
        P(None, "dp", "fsdp"),
        P(None, "dp", "fsdp"),
        P(None, "dp", "fsdp"),
        P("dp", "fsdp"),
        P("dp", "fsdp"),
        P(None, "dp", "fsdp"),
        P(None, "dp", "fsdp"),
        P(None, "dp", "fsdp"),
        P(None, "dp", "fsdp"),
        P("dp", "fsdp"),
    )
    return jax.shard_map(
        per_device,
        mesh=mesh,
        in_specs=placed,
        out_specs=(
            P(),
            P(),
            P("dp", "fsdp"),
            P(None, "dp", "fsdp"),
            P(None, "dp", "fsdp"),
            P(None, "dp", "fsdp"),
            P(None, "dp", "fsdp"),
            P("dp", "fsdp"),
            P("dp", "fsdp"),
            P(None, "dp", "fsdp"),
            P(None, "dp", "fsdp"),
            P(None, "dp", "fsdp"),
            P(None, "dp", "fsdp"),
            P("dp", "fsdp"),
            P("dp", "fsdp"),
            P(None, "dp", "fsdp"),
            P(None, "dp", "fsdp"),
            P(None, "dp", "fsdp"),
            P(None, "dp", "fsdp"),
            P("dp", "fsdp"),
        ),
        check_vma=False,
    )
```
